256 devices in a mesh: row: 32 (over z, x), col: 2 (over core), rep: 4 (over y).
Axes of the slice: x: 4, y: 4, z: 8, core: 2. Of those that a mesh axis runs over, the one named last changes fastest.
Arguments:
- pre_act: bfloat16 [16384, 12288], P(('rep', 'col'), 'row'), may hold values from -8 to 8
- w_out: bfloat16 [12288, 6144], P('row', 'col'), may hold values from -0.0546875 to 0.0546875
- grad_out: bfloat16 [16384, 6144], P(('rep', 'row'), 'col'), may hold values from -6 to 6
Outputs:
- grad_pre: bfloat16 [16384, 12288], P(('rep', 'col'), 'row')
- grad_weight: float32 [12288, 6144], P(('row', 'rep'), 'col')
The draws below stay inside these ranges and needn't reach their ends.
All inputs are finite; a program needn't handle non-finite values.
Results may differ from the reference program's by a relative error of at most 0.0027.
Values may be sent and summed in bfloat16 or wider, within the bound.
A program may use at most 128 MiB of HBM per device.

```python
import jax
import jax.numpy as jnp

D = 6144
FW = 12288
TOKENS = 16384


def level_of(key, extent, shards, least, top_value):
    gain, own = 1.0, jax.random.fold_in(key, 6)
    for axis_at, parts in shards:
        heights = jnp.exp(jax.random.uniform(jax.random.fold_in(own, axis_at), (parts,), jnp.float32, least / len(shards), top_value / len(shards)))
        gain = gain * jnp.repeat(heights, extent[axis_at] // parts).reshape([-1 if axis == axis_at else 1 for axis in range(len(extent))])
    return gain


def scatter_about(stream_key, shape, scale, limit, cuts=(), dtype=jnp.bfloat16):
    values = jax.random.normal(stream_key, shape, jnp.float32) * scale
    if len(cuts) > 0:
        values = level_of(stream_key, shape, cuts, -0.22, 0.18) * values
    return jnp.clip(values, min=-limit, max=limit).astype(dtype)


def setup_inputs(seed: int = 0) -> dict:
    splits = jax.random.split(jax.random.key(seed), 4)
    return {
        "pre_act": scatter_about(splits[0], (TOKENS, FW), 1.5, 8.0, ((0, 8), (1, 32))),
        "w_out": scatter_about(splits[1], (FW, D), FW ** -0.5, 0.0546875, ((0, 32), (1, 2))),
        "grad_out": scatter_about(splits[2], (TOKENS, D), 1.0, 6.0, ((0, 128), (1, 2))),
    }


SQRT_TWO_PI = 0.7978845608028654
CUBIC = 0.044715


def gelu_pair(values):
    inner = SQRT_TWO_PI * (values + CUBIC * values * values * values)
    bent = jnp.tanh(inner)
    output = 0.5 * values * (1.0 + bent)
    slopes = 0.5 * (1.0 + bent) + 0.5 * values * (1.0 - bent * bent) * SQRT_TWO_PI * (1.0 + 3.0 * CUBIC * values * values)
    return output, slopes


def reference(pre_act, w_out, grad_out):
    output, slopes = gelu_pair(pre_act.astype(jnp.float32))
    activation = output.astype(jnp.bfloat16)
    grad_act = jnp.dot(grad_out, w_out.T, preferred_element_type=jnp.float32)
    grad_pre = (grad_act * slopes).astype(jnp.bfloat16)
    grad_weight = jnp.dot(activation.T, grad_out, preferred_element_type=jnp.float32) * (TOKENS ** -0.5)
    return grad_pre, grad_weight
```

```python
import functools

import jax
import jax.numpy as jnp
from jax import lax
from jax.experimental import pallas as pl
from jax.experimental.pallas import tpu as pltpu
from jax.sharding import PartitionSpec as P

SQRT_TWO_PI = 0.7978845608028654
CUBIC = 0.044715
NX, NZ, NY = 4, 8, 4
NSLOT = 2 * NZ
WIDTH = 256
BF16, F32 = jnp.bfloat16, jnp.float32


def gelu_pair(values):
    inner = SQRT_TWO_PI * (values + CUBIC * values * values * values)
    bent = jnp.tanh(inner)
    output = 0.5 * values * (1.0 + bent)
    slopes = 0.5 * (1.0 + bent) + 0.5 * values * (1.0 - bent * bent) * SQRT_TWO_PI * (
        1.0 + 3.0 * CUBIC * values * values
    )
    return output, slopes


def kernel(
    factor,
    pre, w, go, outp, outw,
    G, W, PRE, ACT, SLOPE, GA, GAR, GPS, PF, SA, RA, SB, RB, SX, RX, OUTW,
    rs, gl, wl, wr, prl, prr, acr, gar, gpr, ras, rbs, rxs, ss,
):
    K = G.shape[0]
    rows = go.shape[0]
    hid = pre.shape[1]
    quarter = hid // NY
    half = rows * NZ
    width = G.shape[3]

    row, col, rep = lax.axis_index("row"), lax.axis_index("col"), lax.axis_index("rep")
    z, x = row // NX, lax.rem(row, NX)
    g, xi = x // 2, lax.rem(x, 2)
    up = {"row": lax.rem(z + 1, NZ) * NX + x}
    down = {"row": lax.rem(z + NZ - 1, NZ) * NX + x}
    side = {"row": z * NX + 2 * g + 1 - xi}
    pair = {"row": z * NX + 3 - x}
    core = {"col": 1 - col}
    y1 = rep + 1 - 2 * lax.rem(rep, 2)
    y3 = 3 - rep
    y2 = lax.rem(rep + 2, NY)
    ya, yb = (y1, y3), (y3, y1)

    def same(d):
        return lax.rem(z + NZ + d, NZ) * 2 + xi

    def other(d):
        return lax.rem(z + NZ + d, NZ) * 2 + 1 - xi

    def remote(src, dst, ssem, rsem, dev):
        pltpu.make_async_remote_copy(
            src_ref=src, dst_ref=dst, send_sem=ssem, recv_sem=rsem,
            device_id=dev, device_id_type=pl.DeviceIdType.MESH,
        ).start()

    def arrived(ref, sem):
        pltpu.make_async_copy(ref, ref, sem).wait()

    def cols(c):
        return pl.ds(pl.multiple_of(c * width, width), width)

    def group_rows(zl, group):
        return pl.ds(pl.multiple_of((zl * NX + 2 * group) * rows, 2 * rows), 2 * rows)

    mine = same(0)

    @pl.loop(0, K)
    def _(c):
        pltpu.make_async_copy(go.at[:, cols(c)], G.at[c, mine], gl.at[c]).start()

    for zl in range(NZ // 2):
        pltpu.make_async_copy(
            pre.at[group_rows(zl, g), :], PRE.at[0, pl.ds(zl * 2 * rows, 2 * rows), :], prl.at[0]
        ).start()

    @pl.loop(0, K)
    def _(c):
        pltpu.make_async_copy(w.at[:, cols(c)], W.at[c, pl.ds(0, hid), :], wl.at[c]).start()

    barrier = pltpu.get_barrier_semaphore()
    for dev in (up, down, side, pair, core, {"rep": y1}, {"rep": y3}):
        pl.semaphore_signal(barrier, inc=1, device_id=dev, device_id_type=pl.DeviceIdType.MESH)
    pl.semaphore_wait(barrier, 7)

    for zl in range(NZ // 2):
        remote(
            pre.at[group_rows(zl, 1 - g), :], PRE.at[1, pl.ds(zl * 2 * rows, 2 * rows), :],
            ss.at[4], prr.at[zl], pair,
        )

    @pl.loop(0, K)
    def _(c):
        remote(w.at[:, cols(c)], W.at[c, pl.ds(hid, hid), :], ss.at[3], wr.at[c], pair)

    def forward(c, slot, *ways):
        for way in ways:
            remote(
                G.at[c, slot], G.at[c, slot], ss.at[way], rs.at[c, slot], (up, down, side)[way]
            )

    def landed(c, slot):
        arrived(G.at[c, slot], rs.at[c, slot])

    def stage4(c):
        landed(c, same(-4))
        forward(c, same(-4), 2)

    def stage3(c):
        landed(c, same(-3))
        forward(c, same(-3), 0, 2)
        landed(c, same(3))
        forward(c, same(3), 2)

    def stage2(c):
        landed(c, same(-2))
        forward(c, same(-2), 0, 2)
        landed(c, same(2))
        forward(c, same(2), 1)
        landed(c, other(1))
        forward(c, other(1), 1)

    def stage1(c):
        landed(c, same(-1))
        forward(c, same(-1), 0)
        landed(c, same(1))
        forward(c, same(1), 1)
        landed(c, other(0))
        forward(c, other(0), 0, 1)

    def stage0(c):
        arrived(G.at[c, mine], gl.at[c])
        forward(c, mine, 0, 1, 2)

    def rest(c):
        for slot in (other(-1), other(2), other(-2), other(-3), other(3), other(-4)):
            landed(c, slot)
        arrived(W.at[c, pl.ds(0, hid), :], wl.at[c])
        arrived(W.at[c, pl.ds(hid, hid), :], wr.at[c])

    def activate(h):
        @pl.loop(0, NZ)
        def _(b):
            at = pl.ds(pl.multiple_of(b * rows, rows), rows)
            output, slopes = gelu_pair(PRE[h, at, :].astype(F32))
            SLOPE[at, pl.ds(h * hid, hid)] = slopes
            ACT[col, pl.ds(h * hid, hid), at] = output.T.astype(BF16)

    def send_act(h):
        part = ACT.at[col, pl.ds(h * hid, hid), :]
        remote(part, part, ss.at[5], acr.at[h], core)

    def wait_act():
        for h in range(2):
            part = ACT.at[1 - col, pl.ds(h * hid, hid), :]
            arrived(part, acr.at[h])

    def grad_act(c, s):
        n = NSLOT // 4
        block = G[c, pl.ds(s * n, n)].reshape(n * rows, width)
        at = pl.ds((s % 2) * n * rows, n * rows)
        GA[s // 2, at, :] += lax.dot_general(
            block, W[c], (((1,), (1,)), ((), ())), preferred_element_type=F32
        )

    def grad_w(c, p, s):
        block = G[c, pl.ds(s * NZ, NZ)].reshape(half, width)
        term = jnp.dot(ACT[s], block, preferred_element_type=F32)
        if s == 0:
            PF[p] = term
        else:
            PF[p] += term

    def part_of(p, h, q, m):
        at = pl.ds(pl.multiple_of(h * hid + q * quarter, 8), quarter)
        return PF[p, at, pl.ds(m * 128, 128)]

    def fill_a(c, p):
        for m in range(2):
            for i, q in enumerate((ya[m], y2)):
                for h in range(2):
                    SA[c, m, i, pl.ds(h * quarter, quarter), :] = part_of(p, h, q, m).astype(BF16)

    def send_a(c):
        for m in range(2):
            remote(SA.at[c, m], RA.at[c, m], ss.at[6], ras.at[c, m], {"rep": ya[m]})

    def fill_b(c, p):
        for m in range(2):
            arrived(RA.at[c, m], ras.at[c, m])
            for h in range(2):
                at = pl.ds(h * quarter, quarter)
                total = part_of(p, h, yb[m], m) + RA[c, m, 1, at, :].astype(F32)
                SB[c, m, at, :] = total.astype(BF16)

    def send_b(c):
        for m in range(2):
            remote(SB.at[c, m], RB.at[c, m], ss.at[7], rbs.at[c, m], {"rep": yb[m]})

    def fill_x(c, p):
        for m in range(2):
            arrived(RB.at[c, m], rbs.at[c, m])
            for h in range(2):
                at = pl.ds(h * quarter, quarter)
                total = (
                    part_of(p, h, rep, m)
                    + RA[c, m, 0, at, :].astype(F32)
                    + RB[c, m, at, :].astype(F32)
                )
                if h == 0:
                    OUTW[c, :, pl.ds(m * 128, 128)] = total
                else:
                    SX[c, :, pl.ds(m * 128, 128)] = total.astype(BF16)

    def send_x(c):
        remote(SX.at[c], RX.at[c], ss.at[8], rxs.at[c], pair)

    def finish(c):
        arrived(RX.at[c], rxs.at[c])
        OUTW[c] = (OUTW[c] + RX[c].astype(F32)) * factor

    def write(c):
        pltpu.make_async_copy(OUTW.at[c], outw.at[:, cols(c)], ss.at[12]).start()

    def at_tick(t, lag, body, *more):
        c = t - lag

        @pl.when((c >= 0) & (c < K))
        def _():
            body(c, *more)

    LA = 5
    DEPTH = PF.shape[0]

    def tick(t, carry):
        at_tick(t, 4, stage4)
        at_tick(t, 3, stage3)
        at_tick(t, LA, rest)
        at_tick(t, LA, grad_act, 0)
        at_tick(t, 2, stage2)
        at_tick(t, LA, grad_act, 1)
        at_tick(t, 1, stage1)
        at_tick(t, 0, stage0)
        at_tick(t, LA, grad_act, 2)
        at_tick(t, LA, grad_act, 3)

        @pl.when(t == 1)
        def _():
            GA[...] = jnp.zeros_like(GA)

        @pl.when(t == 2)
        def _():
            arrived(PRE.at[0], prl.at[0])
            activate(0)

        @pl.when(t == 3)
        def _():
            send_act(0)

        @pl.when(t == 4)
        def _():
            for zl in range(NZ // 2):
                arrived(PRE.at[1, pl.ds(zl * 2 * rows, 2 * rows), :], prr.at[zl])
            activate(1)

        @pl.when(t == 5)
        def _():
            send_act(1)
            wait_act()

        p = lax.rem(t + DEPTH - LA, DEPTH)
        at_tick(t, LA, lambda c: grad_w(c, p, 0))
        at_tick(t, LA, lambda c: grad_w(c, p, 1))
        at_tick(t, LA, lambda c: fill_a(c, p))
        at_tick(t, LA + 6, finish)
        at_tick(t, LA + 2, lambda c: fill_b(c, lax.rem(t + 2 * DEPTH - LA - 2, DEPTH)))
        at_tick(t, LA, send_a)
        at_tick(t, LA + 4, lambda c: fill_x(c, lax.rem(t + 2 * DEPTH - LA - 4, DEPTH)))
        at_tick(t, LA + 2, send_b)
        at_tick(t, LA + 6, write)
        at_tick(t, LA + 4, send_x)
        return carry

    lax.fori_loop(0, K + LA, tick, 0)

    piece = 2 * rows
    for s in range(NZ // 2):
        at = pl.ds(s * piece, piece)
        remote(GA.at[1 - col, at, :], GAR.at[at, :], ss.at[9], gar.at[s], core)

    def grad_pre(s):
        at = pl.ds(s * piece, piece)
        arrived(GAR.at[at, :], gar.at[s])
        for h in (1, 0):
            on = pl.ds(h * hid, hid)
            total = (GA[col, at, on] + GAR[at, on]) * SLOPE[at, on]
            GPS[h, at, :] = total.astype(BF16)

    def send_pre(s):
        at = pl.ds(s * piece, piece)
        here = outp.at[group_rows(s, g), :]
        remote(GPS.at[1, at, :], here, ss.at[10], gpr.at[s], pair)
        pltpu.make_async_copy(GPS.at[0, at, :], here, ss.at[11]).start()

    def slot_of(c):
        return c % DEPTH

    fill_b(K - 2, slot_of(K - 2))
    grad_pre(0)
    send_b(K - 2)
    grad_pre(1)
    send_pre(0)
    fill_b(K - 1, slot_of(K - 1))
    send_pre(1)
    send_b(K - 1)
    grad_pre(2)
    fill_x(K - 4, slot_of(K - 4))
    send_pre(2)
    grad_pre(3)
    send_x(K - 4)
    fill_x(K - 3, slot_of(K - 3))
    send_pre(3)
    send_x(K - 3)
    for c in (K - 2, K - 1):
        fill_x(c, slot_of(c))
        send_x(c)
    for c in range(K - 6, K):
        finish(c)
        write(c)

    for s in range(NZ // 2):
        arrived(outp.at[group_rows(s, 1 - g), :], gpr.at[s])
    for way in range(3):
        arrived(G.at[:, pl.ds(0, 5)], ss.at[way])
    arrived(W.at[:, pl.ds(0, hid), :], ss.at[3])
    arrived(PRE.at[1], ss.at[4])
    arrived(ACT.at[col], ss.at[5])
    arrived(SA, ss.at[6])
    arrived(SB, ss.at[7])
    arrived(SX, ss.at[8])
    arrived(GA.at[1 - col], ss.at[9])
    arrived(GPS.at[1], ss.at[10])
    arrived(GPS.at[0], ss.at[11])
    arrived(OUTW, ss.at[12])


def on_device(pre_act, w_out, grad_out):
    rows, feats = grad_out.shape
    tokens, hid = pre_act.shape
    K = feats // WIDTH
    half = rows * NZ
    quarter = hid // NY
    total_tokens = rows * lax.axis_size("row") * lax.axis_size("rep")
    factor = float(total_tokens) ** (-0.5)
    V, DMA = pltpu.VMEM, pltpu.SemaphoreType.DMA
    scratch = [
        V((K, NSLOT, rows, WIDTH), BF16),
        V((K, 2 * hid, WIDTH), BF16),
        V((2, half, hid), BF16),
        V((2, 2 * hid, half), BF16),
        V((half, 2 * hid), F32),
        V((2, half, 2 * hid), F32),
        V((half, 2 * hid), F32),
        V((2, half, hid), BF16),
        V((5, 2 * hid, WIDTH), F32),
        V((K, 2, 2, 2 * quarter, 128), BF16),
        V((K, 2, 2, 2 * quarter, 128), BF16),
        V((K, 2, 2 * quarter, 128), BF16),
        V((K, 2, 2 * quarter, 128), BF16),
        V((K, quarter, WIDTH), BF16),
        V((K, quarter, WIDTH), BF16),
        V((K, quarter, WIDTH), F32),
        DMA((K, NSLOT)), DMA((K,)), DMA((K,)), DMA((K,)), DMA((1,)), DMA((NZ // 2,)),
        DMA((2,)), DMA((NZ // 2,)), DMA((NZ // 2,)), DMA((K, 2)), DMA((K, 2)), DMA((K,)),
        DMA((13,)),
    ]
    anywhere = pl.BlockSpec(memory_space=pl.ANY)
    return pl.pallas_call(
        functools.partial(kernel, factor),
        out_shape=(
            jax.ShapeDtypeStruct((tokens, hid), BF16),
            jax.ShapeDtypeStruct((quarter, feats), F32),
        ),
        in_specs=[anywhere] * 3,
        out_specs=(anywhere, anywhere),
        scratch_shapes=scratch,
        compiler_params=pltpu.CompilerParams(
            collective_id=0, has_side_effects=True, vmem_limit_bytes=60 << 20
        ),
        name="mlp_backward",
    )(pre_act, w_out, grad_out)


def solution(mesh):
    in_specs = (P(("rep", "col"), "row"), P("row", "col"), P(("rep", "row"), "col"))
    out_specs = (P(("rep", "col"), "row"), P(("row", "rep"), "col"))
    return jax.shard_map(
        on_device, mesh=mesh, in_specs=in_specs, out_specs=out_specs, check_vma=False
    )
```

```python
import jax
import jax.numpy as jnp
from jax import lax
from jax.experimental import pallas as pl
from jax.experimental.pallas import tpu as pltpu
from jax.sharding import PartitionSpec as P

SQRT_TWO_PI = 0.7978845608028654
CUBIC = 0.044715
NX, NZ, NY = 4, 8, 4
NSLOT = 2 * NZ
UNIT = 128
SMALL = 0
EARLY = 4
SLOW = 10
LAGS = (0, 2, 3, 4, 5, 6)
BF16, F32 = jnp.bfloat16, jnp.float32


def gelu_pair(values):
    inner = SQRT_TWO_PI * (values + CUBIC * values * values * values)
    bent = jnp.tanh(inner)
    output = 0.5 * values * (1.0 + bent)
    slopes = 0.5 * (1.0 + bent) + 0.5 * values * (1.0 - bent * bent) * SQRT_TWO_PI * (
        1.0 + 3.0 * CUBIC * values * values
    )
    return output, slopes


def kernel(
    pre, w, go, outp, outw, outx,
    G, W, PRE, ACT, SLOPE, GA, GAR, GPS, PF, SA, RA, SB, RB, SX, OUTW,
    rs, gl, wl, wr, prl, prr, acr, gar, gpr, ras, rbs, rxs, ss,
):
    units = G.shape[0]
    K = rs.shape[0]
    BIG = K - SMALL
    rows = go.shape[0]
    hid = pre.shape[1]
    quarter = hid // NY
    half = rows * NZ

    row, col, rep = lax.axis_index("row"), lax.axis_index("col"), lax.axis_index("rep")
    z, x = row // NX, lax.rem(row, NX)
    g, xi = x // 2, lax.rem(x, 2)
    up = {"row": lax.rem(z + 1, NZ) * NX + x}
    down = {"row": lax.rem(z + NZ - 1, NZ) * NX + x}
    side = {"row": z * NX + 2 * g + 1 - xi}
    pair = {"row": z * NX + 3 - x}
    core = {"col": 1 - col}
    y1 = rep + 1 - 2 * lax.rem(rep, 2)
    y3 = 3 - rep
    y2 = lax.rem(rep + 2, NY)

    def same(d):
        return lax.rem(z + NZ + d, NZ) * 2 + xi

    def other(d):
        return lax.rem(z + NZ + d, NZ) * 2 + 1 - xi

    def remote(src, dst, ssem, rsem, dev):
        pltpu.make_async_remote_copy(
            src_ref=src, dst_ref=dst, send_sem=ssem, recv_sem=rsem,
            device_id=dev, device_id_type=pl.DeviceIdType.MESH,
        ).start()

    def arrived(ref, sem):
        pltpu.make_async_copy(ref, ref, sem).wait()

    def cols(u):
        return pl.ds(pl.multiple_of(u * UNIT, UNIT), UNIT)

    def group_rows(zl, group):
        return pl.ds(pl.multiple_of((zl * NX + 2 * group) * rows, 2 * rows), 2 * rows)

    def block_rows(b, group):
        return pl.ds(pl.multiple_of(((b // 2) * NX + 2 * group + b % 2) * rows, rows), rows)

    barrier = pltpu.get_barrier_semaphore()
    for dev in (up, down, side, pair, core, {"rep": y1}, {"rep": y3}):
        pl.semaphore_signal(barrier, inc=1, device_id=dev, device_id_type=pl.DeviceIdType.MESH)

    mine = same(0)

    @pl.loop(0, units)
    def _(u):
        pltpu.make_async_copy(go.at[:, cols(u)], G.at[u, mine], gl.at[u]).start()

    for zl in range(NZ // 2):
        pltpu.make_async_copy(
            pre.at[group_rows(zl, g), :], PRE.at[0, pl.ds(zl * 2 * rows, 2 * rows), :], prl.at[0]
        ).start()

    @pl.loop(0, units)
    def _(u):
        pltpu.make_async_copy(w.at[:, cols(u)], W.at[u, pl.ds(0, hid), :], wl.at[u]).start()

    pl.semaphore_wait(barrier, 7)

    def send_weights(u):
        remote(w.at[:, cols(u)], W.at[u, pl.ds(hid, hid), :], ss.at[3], wr.at[u], pair)

    def send_inputs():
        for u in range(4):
            send_weights(u)
        for zl in range(NZ // 2):
            remote(
                pre.at[group_rows(zl, 1 - g), :], PRE.at[1, pl.ds(zl * 2 * rows, 2 * rows), :],
                ss.at[4], prr.at[zl], pair,
            )
            send_weights(4 + 2 * zl)
            send_weights(5 + 2 * zl)

        @pl.loop(4 + NZ, units)
        def _(u):
            send_weights(u)

    class Chunk:
        def __init__(self, c, u, n):
            self.c, self.u, self.n = c, u, n

        def piece(self, slot):
            return G.at[pl.ds(self.u, self.n), slot]

        def forward(self, slot, *ways):
            for way in ways:
                ref = self.piece(slot)
                remote(ref, ref, ss.at[way], rs.at[self.c, slot], (up, down, side)[way])

        def landed(self, *slots):
            for slot in slots:
                arrived(self.piece(slot), rs.at[self.c, slot])

        def units(self):
            if self.n == 2:
                return [(self.u, 0, 0), (self.u + 1, UNIT, 1)]
            return [(self.u, 0, lax.rem(self.u, 2))]

    def big(c):
        return Chunk(c, 2 * c, 2)

    def small(c):
        return Chunk(c, c + BIG, 1)

    def pass_on(even, odd):
        def body(k):
            for parity, moves in ((0, even), (1, odd)):

                @pl.when(lax.rem(k.c, 2) == parity)
                def _():
                    for slot, *ways in moves:
                        k.landed(slot)
                        k.forward(slot, *ways)

        return body

    stage1 = pass_on(
        ((same(-1), 0, 2), (same(1), 1, 2)),
        ((same(-1), 0), (same(1), 1), (other(0), 0, 1)),
    )
    stage2 = pass_on(
        ((same(-2), 0, 2), (same(2), 1, 2)),
        ((same(-2), 0, 2), (same(2), 1), (other(1), 1)),
    )
    stage3 = pass_on(
        ((same(-3), 0), (other(2), 1), (other(-2), 0)),
        ((same(-3), 0, 2), (same(3), 2)),
    )
    stage4 = pass_on(((other(3), 1),), ((same(-4), 2),))
    kept1 = pass_on(((other(0),),), ())
    kept2 = pass_on(((other(1),), (other(-1),)), ((other(-1),),))
    kept3 = pass_on(((same(3),),), ((other(2),), (other(-2),)))
    kept4 = pass_on(((same(-4),), (other(-3),)), ((other(3),), (other(-3),)))

    def stage0(k):
        for u, _, _ in k.units():
            arrived(G.at[u, mine], gl.at[u])
        k.forward(mine, 0, 1, 2)

    def activate(h):
        @pl.loop(0, NZ)
        def _(b):
            at = pl.ds(pl.multiple_of(b * rows, rows), rows)
            output, slopes = gelu_pair(PRE[h, at, :].astype(F32))
            SLOPE[at, pl.ds(h * hid, hid)] = slopes
            ACT[col, pl.ds(h * hid, hid), at] = output.T.astype(BF16)

    def send_act(h):
        part = ACT.at[col, pl.ds(h * hid, hid), :]
        remote(part, part, ss.at[5], acr.at[h], core)

    def wait_act():
        for h in range(2):
            part = ACT.at[1 - col, pl.ds(h * hid, hid), :]
            arrived(part, acr.at[h])

    first_hop = (same(0), same(-1), same(1), other(0))
    second_hop = (same(-2), same(2), other(1), other(-1))
    third = (same(-3), same(3), other(2), other(-2))
    fourth = (same(-4), other(3), other(-3))
    fifth = (other(-4),)

    def grad_act(k, slots):
        def wide(parts):
            return parts[0] if k.n == 1 else jnp.concatenate(parts, axis=1)

        block = jnp.concatenate([wide([G[k.u + i, s] for i in range(k.n)]) for s in slots], axis=0)
        terms = lax.dot_general(
            block, wide([W[k.u + i] for i in range(k.n)]),
            (((1,), (1,)), ((), ())), preferred_element_type=F32,
        )
        for i, s in enumerate(slots):
            GA[s] += terms[i * rows : (i + 1) * rows]

    def act_first(k):
        kept1(k)
        for u, _, _ in k.units():
            arrived(W.at[u, pl.ds(0, hid), :], wl.at[u])
            arrived(W.at[u, pl.ds(hid, hid), :], wr.at[u])
        grad_act(k, first_hop)

    def act_second(k):
        kept2(k)
        grad_act(k, second_hop)

    def act_third(k):
        kept3(k)
        grad_act(k, third)

    def act_fourth(k):
        kept4(k)
        grad_act(k, fourth)

    def wide_rows(k, slot, n):
        blocks = [G[k.u + i, pl.ds(slot, n)].reshape(n * rows, UNIT) for i in range(k.n)]
        return blocks[0] if k.n == 1 else jnp.concatenate(blocks, axis=1)

    near_half = z // (NZ // 2)
    pairs = NZ // 2

    def far_pair(d):
        return lax.rem(lax.rem(z, pairs) + d, pairs)

    def act_pair(j):
        return ACT[1 - near_half, :, pl.ds(pl.multiple_of(j * 2 * rows, 2 * rows), 2 * rows)]

    def grad_w_most(k, p):
        on = pl.ds(0, k.n * UNIT)
        PF[p, :, on] = jnp.dot(
            ACT[near_half], wide_rows(k, near_half * NZ, NZ), preferred_element_type=F32
        )
        js = [far_pair(d) for d in range(1, pairs)]
        left = jnp.concatenate([act_pair(j) for j in js], axis=1)
        right = jnp.concatenate(
            [wide_rows(k, (1 - near_half) * NZ + 2 * j, 2) for j in js], axis=0
        )
        PF[p, :, on] += jnp.dot(left, right, preferred_element_type=F32)

    def grad_w_last(k, p):
        on = pl.ds(0, k.n * UNIT)
        j = far_pair(0)
        PF[p, :, on] += jnp.dot(
            act_pair(j), wide_rows(k, (1 - near_half) * NZ + 2 * j, 2), preferred_element_type=F32
        )

    def part_of(p, h, q, off):
        at = pl.ds(pl.multiple_of(h * hid + q * quarter, 8), quarter)
        return PF[p, at, pl.ds(off, UNIT)]

    def first(m):
        return y1 + m * (y3 - y1)

    def second(m):
        return y3 + m * (y1 - y3)

    def fill_a(k, p):
        for u, off, m in k.units():
            for i, q in enumerate((first(m), y2)):
                for h in range(2):
                    SA[u, i, pl.ds(h * quarter, quarter), :] = part_of(p, h, q, off).astype(BF16)

    def send_a(k):
        for u, _, m in k.units():
            remote(SA.at[u], RA.at[u], ss.at[6], ras.at[u], {"rep": first(m)})

    def fill_b(k, p):
        for u, off, m in k.units():
            arrived(RA.at[u], ras.at[u])
            for h in range(2):
                at = pl.ds(h * quarter, quarter)
                total = part_of(p, h, second(m), off) + RA[u, 1, at, :].astype(F32)
                SB[u, at, :] = total.astype(BF16)

    def send_b(k):
        for u, _, m in k.units():
            remote(SB.at[u], RB.at[u], ss.at[7], rbs.at[u], {"rep": second(m)})

    def fill_x(k, p):
        for u, off, m in k.units():
            arrived(RB.at[u], rbs.at[u])
            for h in range(2):
                at = pl.ds(h * quarter, quarter)
                total = (
                    part_of(p, h, rep, off)
                    + RA[u, 0, at, :].astype(F32)
                    + RB[u, at, :].astype(F32)
                )
                if h == 0:
                    OUTW[u] = total
                else:
                    SX[u] = total.astype(BF16)

    def send_x(k):
        for u, _, _ in k.units():
            remote(SX.at[u], outx.at[:, cols(u)], ss.at[8], rxs.at[u], pair)
            pltpu.make_async_copy(OUTW.at[u], outw.at[:, cols(u)], ss.at[12]).start()

    def send_sums(slots):
        for s in slots:
            b = s - NZ * (1 - col)

            @pl.when((b >= 0) & (b < NZ))
            def _():
                remote(GA.at[s], GAR.at[b], ss.at[9], gar.at[b], core)

    def on_mine(slots, body):
        for s in slots:
            b = s - NZ * col

            @pl.when((b >= 0) & (b < NZ))
            def _():
                body(s, b)

    def grad_pre(s, b):
        at = pl.ds(pl.multiple_of(b * rows, rows), rows)
        arrived(GAR.at[b], gar.at[b])
        for h in (1, 0):
            on = pl.ds(h * hid, hid)
            total = (GA[s, :, on] + GAR[b, :, on]) * SLOPE[at, on]
            GPS[h, b] = total.astype(BF16)

    def send_pre(s, b):
        here = outp.at[block_rows(b, g), :]
        remote(GPS.at[1, b], here, ss.at[10], gpr.at[b], pair)
        pltpu.make_async_copy(GPS.at[0, b], here, ss.at[11]).start()

    def at_tick(t, lag, body, *more, lo=0, hi=None):
        c = t - lag
        hi = K if hi is None else hi

        @pl.when((c >= lo) & (c < min(hi, BIG)))
        def _():
            body(big(c), *more)

        if hi > BIG:

            @pl.when((c >= BIG) & (c < hi))
            def _():
                body(small(c), *more)

    DEPTH = PF.shape[0]
    L0, L1, L2, L3, L4, LA = LAGS
    groups = ((first_hop, L1), (second_hop, L2), (third, L3), (fourth, L4))

    def tick(t, carry):
        def slot_at(lag):
            return lax.rem(t + 2 * DEPTH - lag, DEPTH)

        def chain(lag, body, slots, lo=0, hi=None):
            more = (slot_at(lag),) if slots else ()
            at_tick(t, lag, body, *more, lo=lo, hi=hi)

        at_tick(t, L0, stage0)
        at_tick(t, L4, stage4)
        at_tick(t, L3, stage3)
        at_tick(t, L4, act_fourth)
        at_tick(t, L2, stage2)
        at_tick(t, L3, act_first, hi=SLOW)
        at_tick(t, L3, act_second, hi=SLOW)
        at_tick(t, L3, act_third)
        at_tick(t, L1, stage1)
        at_tick(t, L2, act_second, lo=SLOW)
        at_tick(t, L1, act_first, lo=SLOW)

        @pl.when(t == 0)
        def _():
            send_inputs()

        @pl.when(t == 1)
        def _():
            GA[...] = jnp.zeros_like(GA)

        @pl.when(t == 3)
        def _():
            arrived(PRE.at[0], prl.at[0])
            activate(0)

        @pl.when(t == 4)
        def _():
            send_act(0)

        @pl.when(t == 8)
        def _():
            for zl in range(NZ // 2):
                arrived(PRE.at[1, pl.ds(zl * 2 * rows, 2 * rows), :], prr.at[zl])
            activate(1)

        @pl.when(t == 9)
        def _():
            send_act(1)
            wait_act()

        for slots, lag in groups:

            @pl.when(t == K - 1 + lag)
            def _():
                send_sums(slots)

        def tail(k):
            k.landed(other(-4))

        at_tick(t, LA, tail)
        chain(LA + 3, grad_w_most, True, 0, EARLY)
        for lag, lo, hi in ((LA + 3, 0, EARLY), (LA, EARLY, None)):
            chain(lag, grad_w_last, True, lo, hi)
            chain(lag, fill_a, True, lo, hi)
        at_tick(t, LA, grad_act, fifth)
        for lag, lo, hi in ((LA + 3, 0, EARLY), (LA, EARLY, None)):
            chain(lag, send_a, False, lo, hi)
        chain(L4, grad_w_most, True, EARLY)

        @pl.when(t == K + LA - 1)
        def _():
            send_sums(fifth)

        for slots, lag in groups:

            @pl.when(t == K + lag)
            def _():
                on_mine(slots, grad_pre)

        for lag, lo, hi in ((LA + 3, 0, EARLY), (LA, EARLY, None)):
            chain(lag + 1, fill_b, True, lo, hi)
            chain(lag + 2, fill_x, True, lo, hi)
            chain(lag + 1, send_b, False, lo, hi)
            chain(lag + 2, send_x, False, lo, hi)

        for slots, lag in groups:

            @pl.when(t == K + lag)
            def _():
                on_mine(slots, send_pre)

        return carry

    lax.fori_loop(0, K + LA, tick, 0)

    def last(c):
        return big(c) if c < BIG else small(c)

    on_mine(fifth, grad_pre)
    fill_x(last(K - 2), (K - 2) % DEPTH)
    fill_b(last(K - 1), (K - 1) % DEPTH)
    on_mine(fifth, send_pre)
    send_x(last(K - 2))
    send_b(last(K - 1))
    fill_x(last(K - 1), (K - 1) % DEPTH)
    send_x(last(K - 1))
    @pl.loop(0, units)
    def _(u):
        arrived(outx.at[:, cols(u)], rxs.at[u])

    for b in range(NZ):
        arrived(outp.at[block_rows(b, 1 - g), :], gpr.at[b])
    for way in range(3):
        arrived(G.at[:, pl.ds(0, 5)], ss.at[way])
    arrived(W.at[:, pl.ds(0, hid), :], ss.at[3])
    arrived(PRE.at[1], ss.at[4])
    arrived(ACT.at[col], ss.at[5])
    arrived(SA, ss.at[6])
    arrived(SB, ss.at[7])
    arrived(SX, ss.at[8])
    arrived(GA.at[pl.ds(0, NZ)], ss.at[9])
    arrived(GPS.at[1], ss.at[10])
    arrived(GPS.at[0], ss.at[11])
    arrived(OUTW, ss.at[12])


def on_device(pre_act, w_out, grad_out):
    rows, feats = grad_out.shape
    tokens, hid = pre_act.shape
    units = feats // UNIT
    K = (units - SMALL) // 2 + SMALL
    half = rows * NZ
    quarter = hid // NY
    total_tokens = rows * lax.axis_size("row") * lax.axis_size("rep")
    factor = float(total_tokens) ** (-0.5)
    V, DMA = pltpu.VMEM, pltpu.SemaphoreType.DMA
    scratch = [
        V((units, NSLOT, rows, UNIT), BF16),
        V((units, 2 * hid, UNIT), BF16),
        V((2, half, hid), BF16),
        V((2, 2 * hid, half), BF16),
        V((half, 2 * hid), F32),
        V((NSLOT, rows, 2 * hid), F32),
        V((NZ, rows, 2 * hid), F32),
        V((2, NZ, rows, hid), BF16),
        V((8, 2 * hid, 2 * UNIT), F32),
        V((units, 2, 2 * quarter, UNIT), BF16),
        V((units, 2, 2 * quarter, UNIT), BF16),
        V((units, 2 * quarter, UNIT), BF16),
        V((units, 2 * quarter, UNIT), BF16),
        V((units, quarter, UNIT), BF16),
        V((units, quarter, UNIT), F32),
        DMA((K, NSLOT)), DMA((units,)), DMA((units,)), DMA((units,)), DMA((1,)),
        DMA((NZ // 2,)), DMA((2,)), DMA((NZ,)), DMA((NZ,)), DMA((units,)), DMA((units,)),
        DMA((units,)), DMA((13,)),
    ]
    anywhere = pl.BlockSpec(memory_space=pl.ANY)
    grad_pre, kept, came = pl.pallas_call(
        kernel,
        out_shape=(
            jax.ShapeDtypeStruct((tokens, hid), BF16),
            jax.ShapeDtypeStruct((quarter, feats), F32),
            jax.ShapeDtypeStruct((quarter, feats), BF16),
        ),
        in_specs=[anywhere] * 3,
        out_specs=(anywhere,) * 3,
        scratch_shapes=scratch,
        compiler_params=pltpu.CompilerParams(
            collective_id=0, has_side_effects=True, vmem_limit_bytes=60 << 20
        ),
        name="mlp_backward",
    )(pre_act, w_out, grad_out)
    return grad_pre, (kept + came.astype(F32)) * factor


def solution(mesh):
    in_specs = (P(("rep", "col"), "row"), P("row", "col"), P(("rep", "row"), "col"))
    out_specs = (P(("rep", "col"), "row"), P(("row", "rep"), "col"))
    return jax.shard_map(
        on_device, mesh=mesh, in_specs=in_specs, out_specs=out_specs, check_vma=False
    )
```

```python
import jax
import jax.numpy as jnp
from jax import lax
from jax.experimental import pallas as pl
from jax.experimental.pallas import tpu as pltpu
from jax.sharding import PartitionSpec as P

SQRT_TWO_PI = 0.7978845608028654
CUBIC = 0.044715
NX, NZ, NY = 4, 8, 4
NSLOT = 2 * NZ
UNIT = 128
SMALL = 0
EARLY = 2
MID, SLOW = 8, 10
LAGS = (0, 2, 3, 4, 5, 6)
BF16, F32 = jnp.bfloat16, jnp.float32


def gelu_pair(values):
    inner = SQRT_TWO_PI * (values + CUBIC * values * values * values)
    bent = jnp.tanh(inner)
    output = 0.5 * values * (1.0 + bent)
    slopes = 0.5 * (1.0 + bent) + 0.5 * values * (1.0 - bent * bent) * SQRT_TWO_PI * (
        1.0 + 3.0 * CUBIC * values * values
    )
    return output, slopes


def kernel(
    pre, w, go, outp, outw, outx,
    G, W, PRE, ACT, SLOPE, GA, GAR, GPS, PF, SA, RA, SB, RB, SX, OUTW,
    rs, gl, wl, wr, prl, prr, acr, gar, gpr, ras, rbs, rxs, ss,
):
    units = G.shape[0]
    K = rs.shape[0]
    BIG = K - SMALL
    rows = go.shape[0]
    hid = pre.shape[1]
    quarter = hid // NY
    half = rows * NZ

    row, col, rep = lax.axis_index("row"), lax.axis_index("col"), lax.axis_index("rep")
    z, x = row // NX, lax.rem(row, NX)
    g, xi = x // 2, lax.rem(x, 2)
    up = {"row": lax.rem(z + 1, NZ) * NX + x}
    down = {"row": lax.rem(z + NZ - 1, NZ) * NX + x}
    side = {"row": z * NX + 2 * g + 1 - xi}
    pair = {"row": z * NX + 3 - x}
    core = {"col": 1 - col}
    y1 = rep + 1 - 2 * lax.rem(rep, 2)
    y3 = 3 - rep
    y2 = lax.rem(rep + 2, NY)

    def same(d):
        return lax.rem(z + NZ + d, NZ) * 2 + xi

    def other(d):
        return lax.rem(z + NZ + d, NZ) * 2 + 1 - xi

    def remote(src, dst, ssem, rsem, dev):
        pltpu.make_async_remote_copy(
            src_ref=src, dst_ref=dst, send_sem=ssem, recv_sem=rsem,
            device_id=dev, device_id_type=pl.DeviceIdType.MESH,
        ).start()

    def arrived(ref, sem):
        pltpu.make_async_copy(ref, ref, sem).wait()

    def cols(u):
        return pl.ds(pl.multiple_of(u * UNIT, UNIT), UNIT)

    def group_rows(zl, group):
        return pl.ds(pl.multiple_of((zl * NX + 2 * group) * rows, 2 * rows), 2 * rows)

    def block_rows(b, group):
        return pl.ds(pl.multiple_of(((b // 2) * NX + 2 * group + b % 2) * rows, rows), rows)

    barrier = pltpu.get_barrier_semaphore()
    for dev in (up, down, side, pair, core, {"rep": y1}, {"rep": y3}):
        pl.semaphore_signal(barrier, inc=1, device_id=dev, device_id_type=pl.DeviceIdType.MESH)

    mine = same(0)

    @pl.loop(0, units)
    def _(u):
        pltpu.make_async_copy(go.at[:, cols(u)], G.at[u, mine], gl.at[u]).start()

    for zl in range(NZ // 2):
        pltpu.make_async_copy(
            pre.at[group_rows(zl, g), :], PRE.at[0, pl.ds(zl * 2 * rows, 2 * rows), :], prl.at[0]
        ).start()

    @pl.loop(0, units)
    def _(u):
        pltpu.make_async_copy(w.at[:, cols(u)], W.at[u, pl.ds(0, hid), :], wl.at[u]).start()

    pl.semaphore_wait(barrier, 7)

    def send_weights(u):
        remote(w.at[:, cols(u)], W.at[u, pl.ds(hid, hid), :], ss.at[3], wr.at[u], pair)

    def send_act_inputs(zl):
        remote(
            pre.at[group_rows(zl, 1 - g), :], PRE.at[1, pl.ds(zl * 2 * rows, 2 * rows), :],
            ss.at[4], prr.at[zl], pair,
        )

    def send_inputs():
        for zl in range(NZ // 2):
            if zl % 2 == 0:
                send_weights(zl)
                send_weights(zl + 1)
            send_act_inputs(zl)

        @pl.loop(NZ // 2, units)
        def _(u):
            send_weights(u)

    class Chunk:
        def __init__(self, c, u, n):
            self.c, self.u, self.n = c, u, n

        def piece(self, slot):
            return G.at[pl.ds(self.u, self.n), slot]

        def forward(self, slot, *ways):
            for way in ways:
                ref = self.piece(slot)
                remote(ref, ref, ss.at[way], rs.at[self.c, slot], (up, down, side)[way])

        def landed(self, *slots):
            for slot in slots:
                arrived(self.piece(slot), rs.at[self.c, slot])

        def units(self):
            if self.n == 2:
                return [(self.u, 0, 0), (self.u + 1, UNIT, 1)]
            return [(self.u, 0, lax.rem(self.u, 2))]

    def big(c):
        return Chunk(c, 2 * c, 2)

    def small(c):
        return Chunk(c, c + BIG, 1)

    def pass_on(even, odd):
        def body(k):
            for parity, moves in ((0, even), (1, odd)):

                @pl.when(lax.rem(k.c, 2) == parity)
                def _():
                    for slot, *ways in moves:
                        k.landed(slot)
                        k.forward(slot, *ways)

        return body

    stage1 = pass_on(
        ((same(-1), 0, 2), (same(1), 1, 2)),
        ((same(-1), 0), (same(1), 1), (other(0), 0, 1)),
    )
    stage2 = pass_on(
        ((same(-2), 0, 2), (same(2), 1, 2)),
        ((same(-2), 0, 2), (same(2), 1), (other(1), 1)),
    )
    stage3 = pass_on(
        ((same(-3), 0), (other(2), 1), (other(-2), 0)),
        ((same(-3), 0, 2), (same(3), 2)),
    )
    stage4 = pass_on(((other(3), 1),), ((same(-4), 2),))
    kept1 = pass_on(((other(0),),), ())
    kept2 = pass_on(((other(1),), (other(-1),)), ((other(-1),),))
    kept3 = pass_on(((same(3),),), ((other(2),), (other(-2),)))
    kept4 = pass_on(((same(-4),), (other(-3),)), ((other(3),), (other(-3),)))

    def stage0(k):
        for u, _, _ in k.units():
            arrived(G.at[u, mine], gl.at[u])
        k.forward(mine, 0, 1, 2)

    def activate(h):
        @pl.loop(0, NZ)
        def _(b):
            at = pl.ds(pl.multiple_of(b * rows, rows), rows)
            output, slopes = gelu_pair(PRE[h, at, :].astype(F32))
            SLOPE[at, pl.ds(h * hid, hid)] = slopes
            ACT[col, pl.ds(h * hid, hid), at] = output.T.astype(BF16)

    def send_act(h):
        part = ACT.at[col, pl.ds(h * hid, hid), :]
        remote(part, part, ss.at[5], acr.at[h], core)

    def wait_act():
        for h in range(2):
            part = ACT.at[1 - col, pl.ds(h * hid, hid), :]
            arrived(part, acr.at[h])

    first_hop = (same(0), same(-1), same(1), other(0))
    second_hop = (same(-2), same(2), other(1), other(-1))
    third = (same(-3), same(3), other(2), other(-2))
    fourth = (same(-4), other(3), other(-3))
    fifth = (other(-4),)

    def grad_act(k, slots):
        def wide(parts):
            return parts[0] if k.n == 1 else jnp.concatenate(parts, axis=1)

        block = jnp.concatenate([wide([G[k.u + i, s] for i in range(k.n)]) for s in slots], axis=0)
        terms = lax.dot_general(
            block, wide([W[k.u + i] for i in range(k.n)]),
            (((1,), (1,)), ((), ())), preferred_element_type=F32,
        )
        for i, s in enumerate(slots):
            GA[s] += terms[i * rows : (i + 1) * rows]

    def act_first(k):
        kept1(k)
        for u, _, _ in k.units():
            arrived(W.at[u, pl.ds(0, hid), :], wl.at[u])
            arrived(W.at[u, pl.ds(hid, hid), :], wr.at[u])
        grad_act(k, first_hop)

    def act_second(k):
        kept2(k)
        grad_act(k, second_hop)

    def act_near(k):
        kept1(k)
        kept2(k)
        for u, _, _ in k.units():
            arrived(W.at[u, pl.ds(0, hid), :], wl.at[u])
            arrived(W.at[u, pl.ds(hid, hid), :], wr.at[u])
        grad_act(k, first_hop + second_hop)

    def act_third(k):
        kept3(k)
        grad_act(k, third)

    def act_fourth(k):
        kept4(k)
        grad_act(k, fourth)

    def wide_rows(k, slot, n):
        blocks = [G[k.u + i, pl.ds(slot, n)].reshape(n * rows, UNIT) for i in range(k.n)]
        return blocks[0] if k.n == 1 else jnp.concatenate(blocks, axis=1)

    near_half = z // (NZ // 2)
    pairs = NZ // 2

    def far_pair(d):
        return lax.rem(lax.rem(z, pairs) + d, pairs)

    def act_pair(j):
        return ACT[1 - near_half, :, pl.ds(pl.multiple_of(j * 2 * rows, 2 * rows), 2 * rows)]

    def grad_w_most(k, p):
        on = pl.ds(0, k.n * UNIT)
        PF[p, :, on] = jnp.dot(
            ACT[near_half], wide_rows(k, near_half * NZ, NZ), preferred_element_type=F32
        )
        js = [far_pair(d) for d in range(1, pairs)]
        left = jnp.concatenate([act_pair(j) for j in js], axis=1)
        right = jnp.concatenate(
            [wide_rows(k, (1 - near_half) * NZ + 2 * j, 2) for j in js], axis=0
        )
        PF[p, :, on] += jnp.dot(left, right, preferred_element_type=F32)

    def grad_w_last(k, p):
        on = pl.ds(0, k.n * UNIT)
        j = far_pair(0)
        PF[p, :, on] += jnp.dot(
            act_pair(j), wide_rows(k, (1 - near_half) * NZ + 2 * j, 2), preferred_element_type=F32
        )

    def part_of(p, h, q, off):
        at = pl.ds(pl.multiple_of(h * hid + q * quarter, 8), quarter)
        return PF[p, at, pl.ds(off, UNIT)]

    def first(m):
        return y1 + m * (y3 - y1)

    def second(m):
        return y3 + m * (y1 - y3)

    def fill_a(k, p):
        for u, off, m in k.units():
            for i, q in enumerate((first(m), y2)):
                for h in range(2):
                    SA[u, i, pl.ds(h * quarter, quarter), :] = part_of(p, h, q, off).astype(BF16)

    def send_a(k):
        for u, _, m in k.units():
            remote(SA.at[u], RA.at[u], ss.at[6], ras.at[u], {"rep": first(m)})

    def fill_b(k, p):
        for u, off, m in k.units():
            arrived(RA.at[u], ras.at[u])
            for h in range(2):
                at = pl.ds(h * quarter, quarter)
                total = part_of(p, h, second(m), off) + RA[u, 1, at, :].astype(F32)
                SB[u, at, :] = total.astype(BF16)

    def send_b(k):
        for u, _, m in k.units():
            remote(SB.at[u], RB.at[u], ss.at[7], rbs.at[u], {"rep": second(m)})

    def fill_x(k, p):
        for u, off, m in k.units():
            arrived(RB.at[u], rbs.at[u])
            for h in range(2):
                at = pl.ds(h * quarter, quarter)
                total = (
                    part_of(p, h, rep, off)
                    + RA[u, 0, at, :].astype(F32)
                    + RB[u, at, :].astype(F32)
                )
                if h == 0:
                    OUTW[u] = total
                else:
                    SX[u] = total.astype(BF16)

    def send_x(k):
        for u, _, _ in k.units():
            remote(SX.at[u], outx.at[:, cols(u)], ss.at[8], rxs.at[u], pair)
            pltpu.make_async_copy(OUTW.at[u], outw.at[:, cols(u)], ss.at[12]).start()

    def send_sums(slots):
        for s in slots:
            b = s - NZ * (1 - col)

            @pl.when((b >= 0) & (b < NZ))
            def _():
                remote(GA.at[s], GAR.at[b], ss.at[9], gar.at[b], core)

    def on_mine(slots, body):
        for s in slots:
            b = s - NZ * col

            @pl.when((b >= 0) & (b < NZ))
            def _():
                body(s, b)

    def grad_pre(s, b):
        at = pl.ds(pl.multiple_of(b * rows, rows), rows)
        arrived(GAR.at[b], gar.at[b])
        for h in (1, 0):
            on = pl.ds(h * hid, hid)
            total = (GA[s, :, on] + GAR[b, :, on]) * SLOPE[at, on]
            GPS[h, b] = total.astype(BF16)

    def send_pre(s, b):
        here = outp.at[block_rows(b, g), :]
        remote(GPS.at[1, b], here, ss.at[10], gpr.at[b], pair)
        pltpu.make_async_copy(GPS.at[0, b], here, ss.at[11]).start()

    def at_tick(t, lag, body, *more, lo=0, hi=None):
        c = t - lag
        hi = K if hi is None else hi

        @pl.when((c >= lo) & (c < min(hi, BIG)))
        def _():
            body(big(c), *more)

        if hi > BIG:

            @pl.when((c >= BIG) & (c < hi))
            def _():
                body(small(c), *more)

    DEPTH = PF.shape[0]
    L0, L1, L2, L3, L4, LA = LAGS
    groups = ((first_hop, L1), (second_hop, L2), (third, L3), (fourth, L4))

    def tick(t, carry):
        def slot_at(lag):
            return lax.rem(t + 2 * DEPTH - lag, DEPTH)

        def chain(lag, body, slots, lo=0, hi=None):
            more = (slot_at(lag),) if slots else ()
            at_tick(t, lag, body, *more, lo=lo, hi=hi)

        at_tick(t, L0, stage0)
        at_tick(t, L4, stage4)
        at_tick(t, L3, stage3)
        at_tick(t, L2, stage2)
        at_tick(t, L1, stage1)
        at_tick(t, L4, act_near, hi=MID)
        at_tick(t, L4, act_third, hi=MID)
        at_tick(t, L3, act_near, lo=MID, hi=SLOW)
        at_tick(t, L4, act_fourth)
        at_tick(t, L3, act_third, lo=MID)
        at_tick(t, L2, act_second, lo=SLOW)
        at_tick(t, L1, act_first, lo=SLOW)

        @pl.when(t == 0)
        def _():
            send_inputs()

        @pl.when(t == 1)
        def _():
            GA[...] = jnp.zeros_like(GA)

        @pl.when(t == 3)
        def _():
            arrived(PRE.at[0], prl.at[0])
            activate(0)

        @pl.when(t == 4)
        def _():
            send_act(0)

        @pl.when(t == 6)
        def _():
            for zl in range(NZ // 2):
                arrived(PRE.at[1, pl.ds(zl * 2 * rows, 2 * rows), :], prr.at[zl])
            activate(1)

        @pl.when(t == 7)
        def _():
            send_act(1)
            wait_act()

        for slots, lag in groups:

            @pl.when(t == K - 1 + lag)
            def _():
                send_sums(slots)

        def tail(k):
            k.landed(other(-4))

        at_tick(t, LA, tail)
        chain(LA + 1, grad_w_most, True, 0, EARLY)
        for lag, lo, hi in ((LA + 1, 0, EARLY), (LA, EARLY, None)):
            chain(lag, grad_w_last, True, lo, hi)
            chain(lag, fill_a, True, lo, hi)
        at_tick(t, LA, grad_act, fifth)
        for lag, lo, hi in ((LA + 1, 0, EARLY), (LA, EARLY, None)):
            chain(lag, send_a, False, lo, hi)
        chain(L4, grad_w_most, True, EARLY)

        @pl.when(t == K + LA - 1)
        def _():
            send_sums(fifth)

        for slots, lag in groups:

            @pl.when(t == K + lag)
            def _():
                on_mine(slots, grad_pre)

        for lag, lo, hi in ((LA + 1, 0, EARLY), (LA, EARLY, None)):
            chain(lag + 1, fill_b, True, lo, hi)
            chain(lag + 2, fill_x, True, lo, hi)
            chain(lag + 1, send_b, False, lo, hi)
            chain(lag + 2, send_x, False, lo, hi)

        for slots, lag in groups:

            @pl.when(t == K + lag)
            def _():
                on_mine(slots, send_pre)

        return carry

    lax.fori_loop(0, K + LA, tick, 0)

    def last(c):
        return big(c) if c < BIG else small(c)

    on_mine(fifth, grad_pre)
    fill_x(last(K - 2), (K - 2) % DEPTH)
    fill_b(last(K - 1), (K - 1) % DEPTH)
    on_mine(fifth, send_pre)
    send_x(last(K - 2))
    send_b(last(K - 1))
    fill_x(last(K - 1), (K - 1) % DEPTH)
    send_x(last(K - 1))
    @pl.loop(0, units)
    def _(u):
        arrived(outx.at[:, cols(u)], rxs.at[u])

    for b in range(NZ):
        arrived(outp.at[block_rows(b, 1 - g), :], gpr.at[b])
    for way in range(3):
        arrived(G.at[:, pl.ds(0, 5)], ss.at[way])
    arrived(W.at[:, pl.ds(0, hid), :], ss.at[3])
    arrived(PRE.at[1], ss.at[4])
    arrived(ACT.at[col], ss.at[5])
    arrived(SA, ss.at[6])
    arrived(SB, ss.at[7])
    arrived(SX, ss.at[8])
    arrived(GA.at[pl.ds(0, NZ)], ss.at[9])
    arrived(GPS.at[1], ss.at[10])
    arrived(GPS.at[0], ss.at[11])
    arrived(OUTW, ss.at[12])


def on_device(pre_act, w_out, grad_out):
    rows, feats = grad_out.shape
    tokens, hid = pre_act.shape
    units = feats // UNIT
    K = (units - SMALL) // 2 + SMALL
    half = rows * NZ
    quarter = hid // NY
    total_tokens = rows * lax.axis_size("row") * lax.axis_size("rep")
    factor = float(total_tokens) ** (-0.5)
    V, DMA = pltpu.VMEM, pltpu.SemaphoreType.DMA
    scratch = [
        V((units, NSLOT, rows, UNIT), BF16),
        V((units, 2 * hid, UNIT), BF16),
        V((2, half, hid), BF16),
        V((2, 2 * hid, half), BF16),
        V((half, 2 * hid), F32),
        V((NSLOT, rows, 2 * hid), F32),
        V((NZ, rows, 2 * hid), F32),
        V((2, NZ, rows, hid), BF16),
        V((8, 2 * hid, 2 * UNIT), F32),
        V((units, 2, 2 * quarter, UNIT), BF16),
        V((units, 2, 2 * quarter, UNIT), BF16),
        V((units, 2 * quarter, UNIT), BF16),
        V((units, 2 * quarter, UNIT), BF16),
        V((units, quarter, UNIT), BF16),
        V((units, quarter, UNIT), F32),
        DMA((K, NSLOT)), DMA((units,)), DMA((units,)), DMA((units,)), DMA((1,)),
        DMA((NZ // 2,)), DMA((2,)), DMA((NZ,)), DMA((NZ,)), DMA((units,)), DMA((units,)),
        DMA((units,)), DMA((13,)),
    ]
    anywhere = pl.BlockSpec(memory_space=pl.ANY)
    grad_pre, kept, came = pl.pallas_call(
        kernel,
        out_shape=(
            jax.ShapeDtypeStruct((tokens, hid), BF16),
            jax.ShapeDtypeStruct((quarter, feats), F32),
            jax.ShapeDtypeStruct((quarter, feats), BF16),
        ),
        in_specs=[anywhere] * 3,
        out_specs=(anywhere,) * 3,
        scratch_shapes=scratch,
        compiler_params=pltpu.CompilerParams(
            collective_id=0, has_side_effects=True, vmem_limit_bytes=60 << 20
        ),
        name="mlp_backward",
    )(pre_act, w_out, grad_out)
    return grad_pre, (kept + came.astype(F32)) * factor


def solution(mesh):
    in_specs = (P(("rep", "col"), "row"), P("row", "col"), P(("rep", "row"), "col"))
    out_specs = (P(("rep", "col"), "row"), P(("row", "rep"), "col"))
    return jax.shard_map(
        on_device, mesh=mesh, in_specs=in_specs, out_specs=out_specs, check_vma=False
    )
```

```python
import jax
import jax.numpy as jnp
from jax import lax
from jax.experimental import pallas as pl
from jax.experimental.pallas import tpu as pltpu
from jax.sharding import PartitionSpec as P

SQRT_TWO_PI = 0.7978845608028654
CUBIC = 0.044715
NX, NZ, NY = 4, 8, 4
NSLOT = 2 * NZ
UNIT = 128
SMALL = 0
EARLY = 2
MID, SLOW = 8, 10
LAGS = (0, 2, 3, 4, 5, 6)
BF16, F32 = jnp.bfloat16, jnp.float32


def gelu_pair(values):
    inner = SQRT_TWO_PI * (values + CUBIC * values * values * values)
    bent = jnp.tanh(inner)
    output = 0.5 * values * (1.0 + bent)
    slopes = 0.5 * (1.0 + bent) + 0.5 * values * (1.0 - bent * bent) * SQRT_TWO_PI * (
        1.0 + 3.0 * CUBIC * values * values
    )
    return output, slopes


def kernel(
    pre, w, go, outp, outw, outx,
    G, W, PRE, ACT, SLOPE, GA, GAR, GPS, PF, SA, RA, SB, RB, SX, OUTW,
    rs, gl, wl, wr, prl, prr, acr, gar, gpr, ras, rbs, rxs, ss,
):
    units = G.shape[0]
    K = rs.shape[0]
    BIG = K - SMALL
    rows = go.shape[0]
    hid = pre.shape[1]
    quarter = hid // NY
    half = rows * NZ

    row, col, rep = lax.axis_index("row"), lax.axis_index("col"), lax.axis_index("rep")
    z, x = row // NX, lax.rem(row, NX)
    g, xi = x // 2, lax.rem(x, 2)
    up = {"row": lax.rem(z + 1, NZ) * NX + x}
    down = {"row": lax.rem(z + NZ - 1, NZ) * NX + x}
    side = {"row": z * NX + 2 * g + 1 - xi}
    pair = {"row": z * NX + 3 - x}
    core = {"col": 1 - col}
    y1 = rep + 1 - 2 * lax.rem(rep, 2)
    y3 = 3 - rep
    y2 = lax.rem(rep + 2, NY)

    def same(d):
        return lax.rem(z + NZ + d, NZ) * 2 + xi

    def other(d):
        return lax.rem(z + NZ + d, NZ) * 2 + 1 - xi

    def remote(src, dst, ssem, rsem, dev):
        pltpu.make_async_remote_copy(
            src_ref=src, dst_ref=dst, send_sem=ssem, recv_sem=rsem,
            device_id=dev, device_id_type=pl.DeviceIdType.MESH,
        ).start()

    def arrived(ref, sem):
        pltpu.make_async_copy(ref, ref, sem).wait()

    def cols(u):
        return pl.ds(pl.multiple_of(u * UNIT, UNIT), UNIT)

    def group_rows(zl, group):
        return pl.ds(pl.multiple_of((zl * NX + 2 * group) * rows, 2 * rows), 2 * rows)

    def block_rows(b, group):
        return pl.ds(pl.multiple_of(((b // 2) * NX + 2 * group + b % 2) * rows, rows), rows)

    barrier = pltpu.get_barrier_semaphore()
    for dev in (up, down, side, pair, core, {"rep": y1}, {"rep": y3}):
        pl.semaphore_signal(barrier, inc=1, device_id=dev, device_id_type=pl.DeviceIdType.MESH)

    mine = same(0)

    @pl.loop(0, units)
    def _(u):
        pltpu.make_async_copy(go.at[:, cols(u)], G.at[u, mine], gl.at[u]).start()

    for zl in range(NZ // 2):
        pltpu.make_async_copy(
            pre.at[group_rows(zl, g), :], PRE.at[0, pl.ds(zl * 2 * rows, 2 * rows), :], prl.at[0]
        ).start()

    @pl.loop(0, units)
    def _(u):
        pltpu.make_async_copy(w.at[:, cols(u)], W.at[u, pl.ds(0, hid), :], wl.at[u]).start()

    pl.semaphore_wait(barrier, 7)

    def send_weights(u):
        remote(w.at[:, cols(u)], W.at[u, pl.ds(hid, hid), :], ss.at[3], wr.at[u], pair)

    def send_act_inputs(zl):
        remote(
            pre.at[group_rows(zl, 1 - g), :], PRE.at[1, pl.ds(zl * 2 * rows, 2 * rows), :],
            ss.at[4], prr.at[zl], pair,
        )

    def send_inputs():
        for zl in range(NZ // 2):
            if zl % 2 == 0:
                send_weights(zl)
                send_weights(zl + 1)
            send_act_inputs(zl)

        @pl.loop(NZ // 2, units)
        def _(u):
            send_weights(u)

    class Chunk:
        def __init__(self, c, u, n):
            self.c, self.u, self.n = c, u, n

        def piece(self, slot):
            return G.at[pl.ds(self.u, self.n), slot]

        def forward(self, slot, *ways):
            for way in ways:
                ref = self.piece(slot)
                remote(ref, ref, ss.at[way], rs.at[self.c, slot], (up, down, side)[way])

        def landed(self, *slots):
            for slot in slots:
                arrived(self.piece(slot), rs.at[self.c, slot])

        def units(self):
            if self.n == 2:
                return [(self.u, 0, 0), (self.u + 1, UNIT, 1)]
            return [(self.u, 0, lax.rem(self.u, 2))]

    def big(c):
        return Chunk(c, 2 * c, 2)

    def small(c):
        return Chunk(c, c + BIG, 1)

    def pass_on(even, odd):
        def body(k):
            for parity, moves in ((0, even), (1, odd)):

                @pl.when(lax.rem(k.c, 2) == parity)
                def _():
                    for slot, *ways in moves:
                        k.landed(slot)
                        k.forward(slot, *ways)

        return body

    stage1 = pass_on(
        ((same(-1), 0, 2), (same(1), 1, 2)),
        ((same(-1), 0), (same(1), 1), (other(0), 0, 1)),
    )
    stage2 = pass_on(
        ((same(-2), 0, 2), (same(2), 1, 2)),
        ((same(-2), 0, 2), (same(2), 1), (other(1), 1)),
    )
    stage3 = pass_on(
        ((same(-3), 0), (other(2), 1), (other(-2), 0)),
        ((same(-3), 0, 2), (same(3), 2)),
    )
    stage4 = pass_on(((other(3), 1),), ((same(-4), 2),))
    kept1 = pass_on(((other(0),),), ())
    kept2 = pass_on(((other(1),), (other(-1),)), ((other(-1),),))
    kept3 = pass_on(((same(3),),), ((other(2),), (other(-2),)))
    kept4 = pass_on(((same(-4),), (other(-3),)), ((other(3),), (other(-3),)))

    def stage0(k):
        for u, _, _ in k.units():
            arrived(G.at[u, mine], gl.at[u])
        k.forward(mine, 0, 1, 2)

    def activate(h):
        @pl.loop(0, NZ)
        def _(b):
            at = pl.ds(pl.multiple_of(b * rows, rows), rows)
            output, slopes = gelu_pair(PRE[h, at, :].astype(F32))
            SLOPE[at, pl.ds(h * hid, hid)] = slopes
            ACT[col, pl.ds(h * hid, hid), at] = output.T.astype(BF16)

    def send_act(h):
        part = ACT.at[col, pl.ds(h * hid, hid), :]
        remote(part, part, ss.at[5], acr.at[h], core)

    def wait_act():
        for h in range(2):
            part = ACT.at[1 - col, pl.ds(h * hid, hid), :]
            arrived(part, acr.at[h])

    first_hop = (same(0), same(-1), same(1), other(0))
    second_hop = (same(-2), same(2), other(1), other(-1))
    third = (same(-3), same(3), other(2), other(-2))
    fourth = (same(-4), other(3), other(-3))
    fifth = (other(-4),)

    def grad_act(k, slots):
        def wide(parts):
            return parts[0] if k.n == 1 else jnp.concatenate(parts, axis=1)

        block = jnp.concatenate([wide([G[k.u + i, s] for i in range(k.n)]) for s in slots], axis=0)
        terms = lax.dot_general(
            block, wide([W[k.u + i] for i in range(k.n)]),
            (((1,), (1,)), ((), ())), preferred_element_type=F32,
        )
        for i, s in enumerate(slots):
            GA[s] += terms[i * rows : (i + 1) * rows]

    def act_first(k):
        kept1(k)
        for u, _, _ in k.units():
            arrived(W.at[u, pl.ds(0, hid), :], wl.at[u])
            arrived(W.at[u, pl.ds(hid, hid), :], wr.at[u])
        grad_act(k, first_hop)

    def act_second(k):
        kept2(k)
        grad_act(k, second_hop)

    def act_near(k):
        kept1(k)
        kept2(k)
        for u, _, _ in k.units():
            arrived(W.at[u, pl.ds(0, hid), :], wl.at[u])
            arrived(W.at[u, pl.ds(hid, hid), :], wr.at[u])
        grad_act(k, first_hop + second_hop)

    def act_third(k):
        kept3(k)
        grad_act(k, third)

    def act_fourth(k):
        kept4(k)
        grad_act(k, fourth)

    def wide_rows(k, slot, n):
        blocks = [G[k.u + i, pl.ds(slot, n)].reshape(n * rows, UNIT) for i in range(k.n)]
        return blocks[0] if k.n == 1 else jnp.concatenate(blocks, axis=1)

    near_half = z // (NZ // 2)
    pairs = NZ // 2

    def far_pair(d):
        return lax.rem(lax.rem(z, pairs) + d, pairs)

    def act_pair(j):
        return ACT[1 - near_half, :, pl.ds(pl.multiple_of(j * 2 * rows, 2 * rows), 2 * rows)]

    def grad_w_most(k, p):
        on = pl.ds(0, k.n * UNIT)
        PF[p, :, on] = jnp.dot(
            ACT[near_half], wide_rows(k, near_half * NZ, NZ), preferred_element_type=F32
        )
        js = [far_pair(d) for d in range(1, pairs)]
        left = jnp.concatenate([act_pair(j) for j in js], axis=1)
        right = jnp.concatenate(
            [wide_rows(k, (1 - near_half) * NZ + 2 * j, 2) for j in js], axis=0
        )
        PF[p, :, on] += jnp.dot(left, right, preferred_element_type=F32)

    def grad_w_last(k, p):
        on = pl.ds(0, k.n * UNIT)
        j = far_pair(0)
        PF[p, :, on] += jnp.dot(
            act_pair(j), wide_rows(k, (1 - near_half) * NZ + 2 * j, 2), preferred_element_type=F32
        )

    def part_of(p, h, q, off):
        at = pl.ds(pl.multiple_of(h * hid + q * quarter, 8), quarter)
        return PF[p, at, pl.ds(off, UNIT)]

    def first(m):
        return y1 + m * (y3 - y1)

    def second(m):
        return y3 + m * (y1 - y3)

    def fill_a(k, p):
        for u, off, m in k.units():
            for i, q in enumerate((first(m), y2)):
                for h in range(2):
                    SA[u, i, pl.ds(h * quarter, quarter), :] = part_of(p, h, q, off).astype(BF16)

    def send_a(k):
        for i in (1, 0):
            for u, _, m in k.units():
                remote(SA.at[u, i], RA.at[u, i], ss.at[6], ras.at[u, i], {"rep": first(m)})

    def fill_b(k, p):
        for u, off, m in k.units():
            arrived(RA.at[u, 1], ras.at[u, 1])
            for h in range(2):
                at = pl.ds(h * quarter, quarter)
                total = part_of(p, h, second(m), off) + RA[u, 1, at, :].astype(F32)
                SB[u, at, :] = total.astype(BF16)

    def send_b(k):
        for u, _, m in k.units():
            remote(SB.at[u], RB.at[u], ss.at[7], rbs.at[u], {"rep": second(m)})

    def fill_x(k, p):
        for u, off, m in k.units():
            arrived(RA.at[u, 0], ras.at[u, 0])
            arrived(RB.at[u], rbs.at[u])
            for h in range(2):
                at = pl.ds(h * quarter, quarter)
                total = (
                    part_of(p, h, rep, off)
                    + RA[u, 0, at, :].astype(F32)
                    + RB[u, at, :].astype(F32)
                )
                if h == 0:
                    OUTW[u] = total
                else:
                    SX[u] = total.astype(BF16)

    def send_x(k):
        for u, _, _ in k.units():
            remote(SX.at[u], outx.at[:, cols(u)], ss.at[8], rxs.at[u], pair)
            pltpu.make_async_copy(OUTW.at[u], outw.at[:, cols(u)], ss.at[12]).start()

    def send_sums(slots):
        for s in slots:
            b = s - NZ * (1 - col)

            @pl.when((b >= 0) & (b < NZ))
            def _():
                remote(GA.at[s], GAR.at[b], ss.at[9], gar.at[b], core)

    def on_mine(slots, body):
        for s in slots:
            b = s - NZ * col

            @pl.when((b >= 0) & (b < NZ))
            def _():
                body(s, b)

    def grad_pre(s, b):
        at = pl.ds(pl.multiple_of(b * rows, rows), rows)
        arrived(GAR.at[b], gar.at[b])
        for h in (1, 0):
            on = pl.ds(h * hid, hid)
            total = (GA[s, :, on] + GAR[b, :, on]) * SLOPE[at, on]
            GPS[h, b] = total.astype(BF16)

    def send_pre(s, b):
        here = outp.at[block_rows(b, g), :]
        remote(GPS.at[1, b], here, ss.at[10], gpr.at[b], pair)
        pltpu.make_async_copy(GPS.at[0, b], here, ss.at[11]).start()

    def at_tick(t, lag, body, *more, lo=0, hi=None):
        c = t - lag
        hi = K if hi is None else hi

        @pl.when((c >= lo) & (c < min(hi, BIG)))
        def _():
            body(big(c), *more)

        if hi > BIG:

            @pl.when((c >= BIG) & (c < hi))
            def _():
                body(small(c), *more)

    DEPTH = PF.shape[0]
    L0, L1, L2, L3, L4, LA = LAGS
    groups = ((first_hop, L1), (second_hop, L2), (third, L3), (fourth, L4))

    def tick(t, carry):
        def slot_at(lag):
            return lax.rem(t + 2 * DEPTH - lag, DEPTH)

        def chain(lag, body, slots, lo=0, hi=None):
            more = (slot_at(lag),) if slots else ()
            at_tick(t, lag, body, *more, lo=lo, hi=hi)

        at_tick(t, L0, stage0)
        at_tick(t, L4, stage4)
        at_tick(t, L3, stage3)
        at_tick(t, L2, stage2)
        at_tick(t, L1, stage1)
        at_tick(t, L4, act_near, hi=MID)
        at_tick(t, L4, act_third, hi=MID)
        at_tick(t, L3, act_near, lo=MID, hi=SLOW)
        at_tick(t, L4, act_fourth)
        at_tick(t, L3, act_third, lo=MID)
        at_tick(t, L2, act_second, lo=SLOW)
        at_tick(t, L1, act_first, lo=SLOW)

        @pl.when(t == 0)
        def _():
            send_inputs()

        @pl.when(t == 1)
        def _():
            GA[...] = jnp.zeros_like(GA)

        @pl.when(t == 3)
        def _():
            arrived(PRE.at[0], prl.at[0])
            activate(0)

        @pl.when(t == 4)
        def _():
            send_act(0)

        @pl.when(t == 6)
        def _():
            for zl in range(NZ // 2):
                arrived(PRE.at[1, pl.ds(zl * 2 * rows, 2 * rows), :], prr.at[zl])
            activate(1)

        @pl.when(t == 7)
        def _():
            send_act(1)
            wait_act()

        for slots, lag in groups:

            @pl.when(t == K - 1 + lag)
            def _():
                send_sums(slots)

        def tail(k):
            k.landed(other(-4))

        at_tick(t, LA, tail)
        chain(LA + 1, grad_w_most, True, 0, EARLY)
        for lag, lo, hi in ((LA + 1, 0, EARLY), (LA, EARLY, None)):
            chain(lag, grad_w_last, True, lo, hi)
            chain(lag, fill_a, True, lo, hi)
        at_tick(t, LA, grad_act, fifth)
        for lag, lo, hi in ((LA + 1, 0, EARLY), (LA, EARLY, None)):
            chain(lag, send_a, False, lo, hi)
        chain(L4, grad_w_most, True, EARLY)

        @pl.when(t == K + LA - 1)
        def _():
            send_sums(fifth)

        for slots, lag in groups:

            @pl.when(t == K + lag)
            def _():
                on_mine(slots, grad_pre)

        for lag, lo, hi in ((LA + 1, 0, EARLY), (LA, EARLY, None)):
            chain(lag + 1, fill_b, True, lo, hi)
            chain(lag + 2, fill_x, True, lo, hi)
            chain(lag + 1, send_b, False, lo, hi)
            chain(lag + 2, send_x, False, lo, hi)

        for slots, lag in groups:

            @pl.when(t == K + lag)
            def _():
                on_mine(slots, send_pre)

        return carry

    lax.fori_loop(0, K + LA, tick, 0)

    def last(c):
        return big(c) if c < BIG else small(c)

    on_mine(fifth, grad_pre)
    fill_x(last(K - 2), (K - 2) % DEPTH)
    fill_b(last(K - 1), (K - 1) % DEPTH)
    on_mine(fifth, send_pre)
    send_x(last(K - 2))
    send_b(last(K - 1))
    fill_x(last(K - 1), (K - 1) % DEPTH)
    send_x(last(K - 1))
    @pl.loop(0, units)
    def _(u):
        arrived(outx.at[:, cols(u)], rxs.at[u])

    for b in range(NZ):
        arrived(outp.at[block_rows(b, 1 - g), :], gpr.at[b])
    for way in range(3):
        arrived(G.at[:, pl.ds(0, 5)], ss.at[way])
    arrived(W.at[:, pl.ds(0, hid), :], ss.at[3])
    arrived(PRE.at[1], ss.at[4])
    arrived(ACT.at[col], ss.at[5])
    arrived(SA, ss.at[6])
    arrived(SB, ss.at[7])
    arrived(SX, ss.at[8])
    arrived(GA.at[pl.ds(0, NZ)], ss.at[9])
    arrived(GPS.at[1], ss.at[10])
    arrived(GPS.at[0], ss.at[11])
    arrived(OUTW, ss.at[12])


def on_device(pre_act, w_out, grad_out):
    rows, feats = grad_out.shape
    tokens, hid = pre_act.shape
    units = feats // UNIT
    K = (units - SMALL) // 2 + SMALL
    half = rows * NZ
    quarter = hid // NY
    total_tokens = rows * lax.axis_size("row") * lax.axis_size("rep")
    factor = float(total_tokens) ** (-0.5)
    V, DMA = pltpu.VMEM, pltpu.SemaphoreType.DMA
    scratch = [
        V((units, NSLOT, rows, UNIT), BF16),
        V((units, 2 * hid, UNIT), BF16),
        V((2, half, hid), BF16),
        V((2, 2 * hid, half), BF16),
        V((half, 2 * hid), F32),
        V((NSLOT, rows, 2 * hid), F32),
        V((NZ, rows, 2 * hid), F32),
        V((2, NZ, rows, hid), BF16),
        V((8, 2 * hid, 2 * UNIT), F32),
        V((units, 2, 2 * quarter, UNIT), BF16),
        V((units, 2, 2 * quarter, UNIT), BF16),
        V((units, 2 * quarter, UNIT), BF16),
        V((units, 2 * quarter, UNIT), BF16),
        V((units, quarter, UNIT), BF16),
        V((units, quarter, UNIT), F32),
        DMA((K, NSLOT)), DMA((units,)), DMA((units,)), DMA((units,)), DMA((1,)),
        DMA((NZ // 2,)), DMA((2,)), DMA((NZ,)), DMA((NZ,)), DMA((units, 2)), DMA((units,)),
        DMA((units,)), DMA((13,)),
    ]
    anywhere = pl.BlockSpec(memory_space=pl.ANY)
    grad_pre, kept, came = pl.pallas_call(
        kernel,
        out_shape=(
            jax.ShapeDtypeStruct((tokens, hid), BF16),
            jax.ShapeDtypeStruct((quarter, feats), F32),
            jax.ShapeDtypeStruct((quarter, feats), BF16),
        ),
        in_specs=[anywhere] * 3,
        out_specs=(anywhere,) * 3,
        scratch_shapes=scratch,
        compiler_params=pltpu.CompilerParams(
            collective_id=0, has_side_effects=True, vmem_limit_bytes=60 << 20
        ),
        name="mlp_backward",
    )(pre_act, w_out, grad_out)
    return grad_pre, (kept + came.astype(F32)) * factor


def solution(mesh):
    in_specs = (P(("rep", "col"), "row"), P("row", "col"), P(("rep", "row"), "col"))
    out_specs = (P(("rep", "col"), "row"), P(("row", "rep"), "col"))
    return jax.shard_map(
        on_device, mesh=mesh, in_specs=in_specs, out_specs=out_specs, check_vma=False
    )
```
